32 devices in a mesh: dp: 2 (over x), expert: 16 (over z, y, core).
Axes of the slice: x: 2, y: 2, z: 4, core: 2. Of those that a mesh axis runs over, the one named last changes fastest.
Arguments:
- tokens: bfloat16 [8192, 1536], P(('dp', 'expert')), may hold values from -6 to 6
- cotangent: bfloat16 [8192, 1536], P(('dp', 'expert')), may hold values from -6 to 6
- routes: int32 [8192, 8], P(('dp', 'expert')), may hold values from 0 to 15, all different within a row; in each aligned block of 256 rows (0 to 255, 256 to 511, ...) at most 192 rows name the same one
- prefix: int32 [32], P(('dp', 'expert')), may hold values from 25 to 128
- w_query: bfloat16 [1536, 1536], P('dp'), may hold values from -0.625 to 0.625
- key_projection: bfloat16 [1536, 512], P('dp'), may hold values from -0.625 to 0.625
- value_projection: bfloat16 [1536, 512], P('dp'), may hold values from -0.625 to 0.625
- w_out: bfloat16 [1536, 1536], P('dp'), may hold values from -0.625 to 0.625
- w_router: bfloat16 [1536, 16], P('dp'), may hold values from -0.078125 to 0.078125
- norm_attn: bfloat16 [1536], P('dp'), may hold values from 0.5 to 1.5
- norm_moe: bfloat16 [1536], P('dp'), may hold values from 0.5 to 1.5
- expert_gate: bfloat16 [16, 1536, 512], P('expert'), may hold values from -0.15625 to 0.15625
- expert_up: bfloat16 [16, 1536, 512], P('expert'), may hold values from -0.3125 to 0.3125
- expert_down: bfloat16 [16, 512, 1536], P('expert'), may hold values from -2 to 2
Outputs:
- out_act: bfloat16 [8192, 1536], P(('dp', 'expert'))
- grad_input: float32 [8192, 1536], P(('dp', 'expert'))
- grad_w_query: float32 [1536, 1536], P('dp')
- grad_w_key: float32 [1536, 512], P('dp')
- grad_w_value: float32 [1536, 512], P('dp')
- grad_w_out: float32 [1536, 1536], P('dp')
- grad_w_router: float32 [1536, 16], P('dp')
- grad_norm_attn: float32 [1536], P('dp')
- grad_norm_moe: float32 [1536], P('dp')
- grad_expert_gate: float32 [16, 1536, 512], P('expert', 'dp')
- grad_expert_up: float32 [16, 1536, 512], P('expert', 'dp')
- grad_expert_down: float32 [16, 512, 1536], P('expert', None, 'dp')
The draws below stay inside these ranges and needn't reach their ends.
Inputs may be any that keep to these rules, and one draw needn't show every extreme that they name: `routes`: each row names 8 different experts; in the rows of one device no expert is named more than 192 times, a bound that some block reaches.
All inputs are finite; a program needn't handle non-finite values.
Results may differ from the reference program's by a relative error of at most 0.023.
Values may be sent and summed in bfloat16 or wider, within the bound.
No kernel may reach another device: no remote copies, remote signals or barrier semaphores. Data moves between devices by JAX's collectives and lax.ppermute only.
A program may use at most 256 MiB of HBM per device.

```python
import math
import jax
import jax.numpy as jnp
import numpy as np
from jax import lax

MODEL_WIDTH = 1536
QUERY_HEADS = 24
KEY_VALUE_HEADS = 8
HEAD_SIZE = 64
FFE = 512
TOP = 8
DEVICE_TOKENS = 256
EXPERTS = 16
MOST = 192
SEQUENCES = 32
TOKENS = 8192


def set_ends(entries, stream_key, low, high):
    spot = [jax.random.randint(jax.random.fold_in(stream_key, axis), (), 0, length) for axis, length in enumerate(entries.shape)]
    longest = entries.shape.index(max(entries.shape))
    beside = spot[:longest] + [(spot[longest] + 1) % entries.shape[longest]] + spot[longest + 1:]
    return entries.at[tuple(spot)].set(low).at[tuple(beside)].set(high)


def block_levels(key, extent, split, smallest, top_value):
    level, own = 1.0, jax.random.fold_in(key, 6)
    for axis_at, blocks in split:
        steps = jnp.exp(jax.random.uniform(jax.random.fold_in(own, axis_at), (blocks,), jnp.float32, smallest / len(split), top_value / len(split)))
        level = level * jnp.repeat(steps, extent[axis_at] // blocks).reshape([-1 if axis == axis_at else 1 for axis in range(len(extent))])
    return level


def shared_out(own_key, own, number, rows, count, top, bound, lean):
    order = jax.random.permutation(own_key, count)
    packed, usual = shares(count, rows * top, bound, lean, True), shares(count, rows * top, bound, lean, False)
    places = jnp.arange(count)

    def named(tallies, turn):
        used = int((tallies > 0).sum())
        fixed = max(1, used // 4)
        shifted = fixed + (places - fixed + turn * (used - fixed)) % max(1, count - fixed)
        return jnp.zeros((count,), jnp.int32).at[order[jnp.where(places < fixed, places, shifted)]].set(jnp.asarray(tallies, jnp.int32))

    tallies = jnp.where(number % 4 == 0, named(packed, number // 4), named(usual, number - number // 4 - 1))
    mixed = jax.random.permutation(jax.random.fold_in(own, 3), count)
    source_of, receiver = mixed[0:count // 2 * 2:2], mixed[1:count // 2 * 2:2]
    room = jnp.minimum(tallies[source_of] - 1, bound - tallies[receiver]) // 2
    room = jnp.where((source_of == order[0]) | (receiver == order[0]) | (tallies[receiver] == 0), 0, jnp.maximum(room, 0))
    shifted = jax.random.randint(jax.random.fold_in(own, 4), (count // 2,), 0, 1 << 20) % (room + 1)
    tallies = tallies.at[source_of].add(-shifted).at[receiver].add(shifted)
    items = jnp.searchsorted(jnp.cumsum(tallies), jnp.arange(rows * top), side="right").astype(jnp.int32)
    table = items.reshape(top, rows).T
    table = table[jax.random.permutation(jax.random.fold_in(own, 1), rows)]
    turn = jax.random.randint(jax.random.fold_in(own, 2), (rows, 1), 0, top)
    return jnp.take_along_axis(table, (jnp.arange(top)[None, :] + turn) % top, axis=1)


def shares(amount, total, most, lean, full):
    weights = [(1 << 20) // math.isqrt(rank ** lean) + 1 for rank in range(1, amount + 1)]
    largest = most if full else min(most, max(-(-total // amount), total * weights[0] // sum(weights)))
    least = 1 if total - largest >= amount - 1 else 0
    given, surplus = [largest] + [least] * (amount - 1), total - largest - least * (amount - 1)
    while surplus > 0:
        free = [i for i in range(1, amount) if given[i] < largest] or [i for i in range(1, amount) if given[i] < most]
        pool, remaining = sum([weights[i] for i in free]), surplus
        for i in free:
            addition = min(most - given[i], max(1, remaining * weights[i] // pool), surplus)
            given[i] = given[i] + addition
            surplus = surplus - addition
    return np.array(given)


def scatter_about(key, dims, spread, most, pieces=(), kind=jnp.bfloat16):
    values = jax.random.normal(key, dims, jnp.float32) * spread
    if len(pieces) > 0:
        values = block_levels(key, dims, pieces, -0.22, 0.18) * values
    return jnp.clip(values, min=-most, max=most).astype(kind)


def setup_inputs(seed: int = 0) -> dict:
    key_list = jax.random.split(jax.random.key(seed), 15)
    tokens = scatter_about(key_list[0], (TOKENS, MODEL_WIDTH), 1.0, 6.0, ((0, 32),))
    cotangent = scatter_about(key_list[1], (TOKENS, MODEL_WIDTH), 1.0, 6.0, ((0, 32),))
    routes_keys = jax.random.split(jax.random.fold_in(key_list[2], 1), TOKENS // DEVICE_TOKENS)
    routes_turns = jax.random.permutation(jax.random.fold_in(key_list[2], 3), TOKENS // DEVICE_TOKENS)
    routes = jax.vmap(lambda own, number: shared_out(jax.random.fold_in(key_list[2], 2), own, number, DEVICE_TOKENS, EXPERTS, TOP, MOST, 2))(routes_keys, routes_turns).reshape((TOKENS, TOP))
    prefix = set_ends(jax.random.randint(key_list[3], (SEQUENCES,), DEVICE_TOKENS // 10, DEVICE_TOKENS // 2 + 1), jax.random.fold_in(key_list[3], 1), DEVICE_TOKENS // 10, (DEVICE_TOKENS // 2 + 1) - 1).astype(jnp.int32)
    w_query = scatter_about(key_list[4], (MODEL_WIDTH, QUERY_HEADS * HEAD_SIZE), (MODEL_WIDTH // 16) ** -0.5, 0.625, ((0, 2),))
    key_projection = scatter_about(key_list[5], (MODEL_WIDTH, KEY_VALUE_HEADS * HEAD_SIZE), (MODEL_WIDTH // 16) ** -0.5, 0.625, ((0, 2),))
    value_projection = scatter_about(key_list[6], (MODEL_WIDTH, KEY_VALUE_HEADS * HEAD_SIZE), (MODEL_WIDTH // 16) ** -0.5, 0.625, ((0, 2),))
    w_out = scatter_about(key_list[7], (QUERY_HEADS * HEAD_SIZE, MODEL_WIDTH), (QUERY_HEADS * HEAD_SIZE // 16) ** -0.5, 0.625, ((0, 2),))
    w_router = scatter_about(key_list[8], (MODEL_WIDTH, EXPERTS), (4 * MODEL_WIDTH) ** -0.5, 0.078125, ((0, 2),))
    norm_attn = jnp.clip(1.0 + 0.1 * jax.random.normal(key_list[9], (MODEL_WIDTH,), jnp.float32), 0.5, 1.5).astype(jnp.bfloat16)
    norm_moe = jnp.clip(1.0 + 0.1 * jax.random.normal(key_list[10], (MODEL_WIDTH,), jnp.float32), 0.5, 1.5).astype(jnp.bfloat16)
    expert_gate = scatter_about(key_list[11], (EXPERTS, MODEL_WIDTH, FFE), MODEL_WIDTH ** -0.5, 0.15625, ((0, 16),))
    expert_up = scatter_about(key_list[12], (EXPERTS, MODEL_WIDTH, FFE), (MODEL_WIDTH // 4) ** -0.5, 0.3125, ((0, 16),))
    expert_down = scatter_about(key_list[13], (EXPERTS, FFE, MODEL_WIDTH), (max(FFE // 64, 1)) ** -0.5, 2.0, ((0, 16),))
    return dict(tokens=tokens, cotangent=cotangent, routes=routes, prefix=prefix, w_query=w_query, key_projection=key_projection, value_projection=value_projection, w_out=w_out, w_router=w_router, norm_attn=norm_attn, norm_moe=norm_moe, expert_gate=expert_gate, expert_up=expert_up, expert_down=expert_down)


eps_norm = 1e-06
att_scale = 0.015625
branch_scale = 0.22
rope_base = 10000.0

@jax.custom_vjp
def narrow_cast(v):
    return lax.optimization_barrier(v.astype(jnp.bfloat16)).astype(jnp.float32)

@jax.custom_vjp
def narrow_cast_reverse(v):
    return v

def low_keep(v):
    return (narrow_cast(v), None)

def low_pass(kept, grad):
    return (grad,)

def back_keep(v):
    return (v, None)

def back_low(kept, grad):
    return (narrow_cast(grad),)
narrow_cast.defvjp(low_keep, low_pass)
narrow_cast_reverse.defvjp(back_keep, back_low)

def rotation(sequence_length, head_dim):
    half = head_dim // 2
    places = jnp.arange(sequence_length).astype(jnp.float32)[:, None]
    freqs = rope_base ** (-2.0 * jnp.arange(half).astype(jnp.float32) / head_dim)
    angles = places * freqs[None, :]
    return (jnp.cos(angles)[:, None, :], jnp.sin(angles)[:, None, :])

def apply_rotary(values, cosine_table, sine_table):
    half = values.shape[-1] // 2
    first = values[..., :half]
    second = values[..., half:]
    return jnp.concatenate([first * cosine_table - second * sine_table, second * cosine_table + first * sine_table], axis=-1)

def matrix_product(left, right):
    return jnp.dot(left, right, precision=lax.Precision.HIGHEST, preferred_element_type=jnp.float32)

def reference(tokens, cotangent, routes, prefix, w_query, key_projection, value_projection, w_out, w_router, norm_attn, norm_moe, expert_gate, expert_up, expert_down):
    count = tokens.shape[0]
    sequence_batch = count // DEVICE_TOKENS
    query_group_size = QUERY_HEADS // KEY_VALUE_HEADS
    cosine_table, sine_table = rotation(DEVICE_TOKENS, HEAD_SIZE)
    member_table = (routes[:, :, None] == jnp.arange(EXPERTS, dtype=jnp.int32)[None, None, :]).astype(jnp.float32)

    def one_sequence(item):
        query_part, key_part, value_part, limit = item
        query_place = jnp.arange(DEVICE_TOKENS, dtype=jnp.int32)[:, None]
        key_place = jnp.arange(DEVICE_TOKENS, dtype=jnp.int32)[None, :]
        allowed = (key_place <= query_place) | (key_place < limit)
        scores = narrow_cast_reverse(jnp.einsum('qhgd,khd->hgqk', query_part, key_part, precision=lax.Precision.HIGHEST) * att_scale)
        scores = jnp.where(allowed, scores, -1e+30)
        probs = jax.nn.softmax(scores, axis=-1)
        return jnp.einsum('hgqk,khd->qhgd', narrow_cast(probs), value_part, precision=lax.Precision.HIGHEST)

    def forward(inputs, query_w, key_matrix, value_matrix, out_w, router_w, gain_one, gain_two, gate_w, up_w, down_w):
        scale_one = lax.rsqrt(lax.optimization_barrier(jnp.mean(inputs * inputs, axis=1, keepdims=True)) + eps_norm)
        first_normalized = narrow_cast(inputs * scale_one * gain_one)
        query_linear = narrow_cast_reverse(matrix_product(first_normalized, query_w)).reshape(sequence_batch, DEVICE_TOKENS, QUERY_HEADS, HEAD_SIZE)
        key_linear = narrow_cast_reverse(matrix_product(first_normalized, key_matrix)).reshape(sequence_batch, DEVICE_TOKENS, KEY_VALUE_HEADS, HEAD_SIZE)
        value_rows_every = narrow_cast(narrow_cast_reverse(matrix_product(first_normalized, value_matrix))).reshape(sequence_batch, DEVICE_TOKENS, KEY_VALUE_HEADS, HEAD_SIZE)
        query_rows = narrow_cast(apply_rotary(query_linear, cosine_table, sine_table)).reshape(sequence_batch, DEVICE_TOKENS, KEY_VALUE_HEADS, query_group_size, HEAD_SIZE)
        keys_rot = narrow_cast(apply_rotary(key_linear, cosine_table, sine_table))
        attended = lax.map(jax.checkpoint(one_sequence), (query_rows, keys_rot, value_rows_every, prefix))
        attended = narrow_cast(narrow_cast_reverse(attended.reshape(count, QUERY_HEADS * HEAD_SIZE)))
        after_attn = inputs + branch_scale * narrow_cast_reverse(matrix_product(attended, out_w))
        scale_two = lax.rsqrt(lax.optimization_barrier(jnp.mean(after_attn * after_attn, axis=1, keepdims=True)) + eps_norm)
        normed_two = narrow_cast(after_attn * scale_two * gain_two)
        logits = matrix_product(normed_two, router_w)
        chosen = lax.optimization_barrier(jnp.sum(member_table * logits[:, None, :], axis=2))
        gates = jax.nn.softmax(chosen, axis=1)
        mixing = lax.optimization_barrier(jnp.sum(member_table * gates[:, :, None], axis=1))

        def one_expert(total, item):
            gate_e, up_e, down_e, weight = item
            entry = narrow_cast_reverse(normed_two)
            gate_pre = narrow_cast_reverse(matrix_product(entry, gate_e))
            up_pre = narrow_cast_reverse(matrix_product(entry, up_e))
            hidden = narrow_cast(jax.nn.silu(gate_pre) * up_pre)
            output = narrow_cast(narrow_cast_reverse(matrix_product(hidden, down_e)))
            return (total + weight[:, None] * output, None)
        start = jnp.zeros((count, MODEL_WIDTH), jnp.float32)
        mixture, unused = lax.scan(jax.checkpoint(one_expert), start, (gate_w, up_w, down_w, mixing.T))
        return after_attn + branch_scale * mixture
    primals = (tokens.astype(jnp.float32), w_query.astype(jnp.float32), key_projection.astype(jnp.float32), value_projection.astype(jnp.float32), w_out.astype(jnp.float32), w_router.astype(jnp.float32), norm_attn.astype(jnp.float32), norm_moe.astype(jnp.float32), expert_gate.astype(jnp.float32), expert_up.astype(jnp.float32), expert_down.astype(jnp.float32))
    result, pullback = jax.vjp(forward, *primals)
    grads = pullback(cotangent.astype(jnp.float32))
    return (result.astype(jnp.bfloat16), grads[0], grads[1], grads[2], grads[3], grads[4], grads[5], grads[6], grads[7], grads[8], grads[9], grads[10])
```

```python
import jax
import jax.numpy as jnp
from jax import lax
from jax.sharding import PartitionSpec as P

QUERY_HEADS = 24
KEY_VALUE_HEADS = 8
HEAD_SIZE = 64
TOP = 8
RING = 4

eps_norm = 1e-06
att_scale = 0.015625
branch_scale = 0.22
rope_base = 10000.0


def rotation(sequence_length, head_dim):
    half = head_dim // 2
    places = jnp.arange(sequence_length).astype(jnp.float32)[:, None]
    freqs = rope_base ** (-2.0 * jnp.arange(half).astype(jnp.float32) / head_dim)
    angles = places * freqs[None, :]
    return (jnp.cos(angles)[:, None, :], jnp.sin(angles)[:, None, :])


def apply_rotary(values, cosine_table, sine_table):
    half = values.shape[-1] // 2
    first = values[..., :half]
    second = values[..., half:]
    return jnp.concatenate(
        [first * cosine_table - second * sine_table, second * cosine_table + first * sine_table],
        axis=-1,
    )


def reverse_rotary(grads, cosine_table, sine_table):
    half = grads.shape[-1] // 2
    first = grads[..., :half]
    second = grads[..., half:]
    return jnp.concatenate(
        [first * cosine_table + second * sine_table, second * cosine_table - first * sine_table],
        axis=-1,
    )


def masked_scores(query_groups, keys_rot, allowed):
    scores = (
        jnp.einsum("qhgd,khd->hgqk", query_groups, keys_rot, preferred_element_type=jnp.float32)
        * att_scale
    )
    return jnp.where(allowed, scores, -1e30)


def dot(a, b):
    return jnp.dot(a, b, preferred_element_type=jnp.float32)


def dot_t(a, b):
    return lax.dot_general(a, b, (((1,), (1,)), ((), ())), preferred_element_type=jnp.float32)


def t_dot(a, b):
    return lax.dot_general(a, b, (((0,), (0,)), ((), ())), preferred_element_type=jnp.float32)


def low(x):
    return x.astype(jnp.bfloat16)


def wide(x):
    return x.astype(jnp.float32)


def two_parts(x):
    high = low(x)
    return jnp.concatenate([high, low(x - wide(high))], axis=1)


class Layout:
    def __init__(self):
        self.experts = lax.axis_size("expert")
        self.dp = lax.axis_size("dp")
        self.sides = self.experts // (2 * RING)
        self.index = lax.axis_index("expert")
        self.dp_index = lax.axis_index("dp")
        self.core = self.index % 2
        self.side = (self.index // 2) % self.sides
        self.ring = self.index // (2 * self.sides)

    def place(self, ring, side, core):
        return ((ring % RING) * self.sides + side % self.sides) * 2 + core

    def _perm(self, ring, side):
        n = self.experts
        pairs = []
        for i in range(n):
            core, s, r = i % 2, (i // 2) % self.sides, i // (2 * self.sides)
            pairs.append((i, self.place(r + ring, s + side, core)))
        return pairs

    def next_ring(self, x):
        return lax.ppermute(x, "expert", self._perm(1, 0))

    def next_side(self, x):
        return lax.ppermute(x, "expert", self._perm(0, 1))

    def other_core(self, x):
        return lax.ppermute(x, "expert", [(i, i ^ 1) for i in range(self.experts)])

    def next_dp(self, x, step):
        n = self.dp
        return lax.ppermute(x, "dp", [(i, (i + step) % n) for i in range(n)])

    def spread(self, x):
        blocks = []
        for s in range(RING):
            row = [x]
            for _ in range(self.sides - 1):
                row.append(self.next_side(row[-1]))
            blocks.append(row)
            if s < RING - 1:
                x = self.next_ring(x)
        return blocks

    def collect(self, parts, cast):
        total = None
        for s in list(range(1, RING)) + [0]:
            row = parts[s]
            acc = None
            for t in list(range(1, self.sides)) + [0]:
                acc = row[t] if acc is None else wide(self.next_side(cast(acc))) + row[t]
            total = acc if total is None else wide(self.next_ring(cast(total))) + acc
        return total


def weight_pieces(lay, w):
    rows, columns = w.shape
    half = rows // 2
    pieces = [(lay.dp_index * rows, w)]
    mine = lax.dynamic_slice(w, (lay.core * half, 0), (half, columns))
    for step in range(1, lay.dp):
        source = (lay.dp_index - step) % lay.dp
        got = lay.next_dp(mine, step)
        rest = lay.other_core(got)
        pieces.append((source * rows + lay.core * half, got))
        pieces.append((source * rows + (1 - lay.core) * half, rest))
    return pieces


def through(x, pieces):
    total = None
    for offset, w in pieces:
        part = dot(lax.dynamic_slice(x, (0, offset), (x.shape[0], w.shape[0])), w)
        total = part if total is None else total + part
    return total


def back_through(y, pieces, width):
    out = jnp.zeros((y.shape[0], width), jnp.float32)
    for offset, w in pieces:
        out = lax.dynamic_update_slice(out, dot_t(y, w), (0, offset))
    return out


def features_of(lay, x, step):
    rows = x.shape[1] // lay.dp
    return lax.dynamic_slice(x, (0, ((lay.dp_index + step) % lay.dp) * rows), (x.shape[0], rows))


def over_dp(lay, left, right):
    total = t_dot(features_of(lay, left, 0), right)
    for step in range(1, lay.dp):
        other_left = lay.next_dp(features_of(lay, left, step), step)
        other_right = lay.next_dp(right, step)
        total = total + t_dot(other_left, other_right)
    return total


def scatter_dp(lay, x, axis):
    size = x.shape[axis] // lay.dp

    def part(step):
        start = ((lay.dp_index + step) % lay.dp) * size
        return lax.dynamic_slice_in_dim(x, start, size, axis)

    total = wide(part(0))
    for step in range(1, lay.dp):
        total = total + wide(lay.next_dp(low(part(step)), step))
    return total


def dense_gates(routes, logits):
    experts = logits.shape[1]
    member = jnp.any(
        routes[:, :, None] == jnp.arange(experts, dtype=jnp.int32)[None, None, :], axis=1
    )
    masked = jnp.where(member, logits, -jnp.inf)
    unnormed = jnp.where(member, jnp.exp(logits - jnp.max(masked, axis=1, keepdims=True)), 0.0)
    return unnormed / jnp.sum(unnormed, axis=1, keepdims=True)


def body(
    tokens,
    cotangent,
    routes,
    prefix,
    w_query,
    key_projection,
    value_projection,
    w_out,
    w_router,
    norm_attn,
    norm_moe,
    expert_gate,
    expert_up,
    expert_down,
):
    lay = Layout()
    sequence_length, width = tokens.shape
    experts = lay.experts
    group = QUERY_HEADS // KEY_VALUE_HEADS
    rows = w_query.shape[0]

    small = jnp.concatenate([w_router, norm_attn[:, None], norm_moe[:, None]], axis=1)
    small_full = jnp.zeros((rows * lay.dp, small.shape[1]), jnp.bfloat16)
    small_full = lax.dynamic_update_slice(small_full, small, (lay.dp_index * rows, 0))
    for step in range(1, lay.dp):
        source = (lay.dp_index - step) % lay.dp
        small_full = lax.dynamic_update_slice(
            small_full, lay.next_dp(small, step), (source * rows, 0)
        )
    router_full = small_full[:, :experts]
    gain_one = wide(small_full[:, experts])[None, :]
    gain_two = wide(small_full[:, experts + 1])[None, :]
    qkv_pieces = weight_pieces(
        lay, jnp.concatenate([w_query, key_projection, value_projection], axis=1)
    )
    out_pieces = weight_pieces(lay, w_out)

    gate_w = jnp.concatenate([expert_gate[0], lay.other_core(expert_gate[0])], axis=1)
    up_w = jnp.concatenate([expert_up[0], lay.other_core(expert_up[0])], axis=1)
    down_w = jnp.concatenate([expert_down[0], lay.other_core(expert_down[0])], axis=0)

    routes_blocks = lay.spread(routes)
    cot_blocks = lay.spread(cotangent)

    cosine_table, sine_table = rotation(sequence_length, HEAD_SIZE)
    tokens_float = wide(tokens)
    scale_one = lax.rsqrt(jnp.mean(tokens_float * tokens_float, axis=1, keepdims=True) + eps_norm)
    first_normalized = low(tokens_float * scale_one * gain_one)
    linear = through(first_normalized, qkv_pieces)
    q_width = QUERY_HEADS * HEAD_SIZE
    kv_width = KEY_VALUE_HEADS * HEAD_SIZE
    query_linear = linear[:, :q_width].reshape(sequence_length, QUERY_HEADS, HEAD_SIZE)
    key_linear = linear[:, q_width : q_width + kv_width].reshape(
        sequence_length, KEY_VALUE_HEADS, HEAD_SIZE
    )
    value_rows_every = low(linear[:, q_width + kv_width :]).reshape(
        sequence_length, KEY_VALUE_HEADS, HEAD_SIZE
    )
    query_groups = low(apply_rotary(query_linear, cosine_table, sine_table)).reshape(
        sequence_length, KEY_VALUE_HEADS, group, HEAD_SIZE
    )
    keys_rot = low(apply_rotary(key_linear, cosine_table, sine_table))
    query_place = jnp.arange(sequence_length)[:, None]
    key_place = jnp.arange(sequence_length)[None, :]
    allowed = (key_place <= query_place) | (key_place < prefix[0])
    scores = masked_scores(query_groups, keys_rot, allowed)
    highest = jnp.max(scores, axis=-1, keepdims=True)
    unnormed = jnp.exp(scores - highest)
    total = jnp.sum(unnormed, axis=-1, keepdims=True)
    log_total = highest + jnp.log(total)
    probs_low = low(unnormed / total)
    attended = jnp.einsum(
        "hgqk,khd->qhgd", probs_low, value_rows_every, preferred_element_type=jnp.float32
    )
    attended_low = low(attended.reshape(sequence_length, q_width))
    after_attn = tokens_float + branch_scale * through(attended_low, out_pieces)
    scale_two = lax.rsqrt(jnp.mean(after_attn * after_attn, axis=1, keepdims=True) + eps_norm)
    normed_two = low(after_attn * scale_two * gain_two)

    gates = dense_gates(routes, dot(normed_two, router_full))
    h2_blocks = lay.spread(normed_two)
    ids = jnp.arange(experts, dtype=jnp.int32)
    own_expert = (ids == lay.index).astype(jnp.float32)
    other_expert = (ids == lay.index + 1 - 2 * lay.core).astype(jnp.float32)
    ffe = expert_gate.shape[2]

    mix_parts, entry_parts, gate_parts = [], [], []
    kept = []
    for s in range(RING):
        mix_row, entry_row, gate_row = [], [], []
        for t in range(lay.sides):
            h2, cot = h2_blocks[s][t], cot_blocks[s][t]
            block_gates = dense_gates(routes_blocks[s][t], dot(h2, router_full))
            weight_own = jnp.sum(block_gates * own_expert[None, :], axis=1, keepdims=True)
            weight_other = jnp.sum(block_gates * other_expert[None, :], axis=1, keepdims=True)
            weight = jnp.concatenate(
                [
                    jnp.broadcast_to(weight_own, (sequence_length, ffe)),
                    jnp.broadcast_to(weight_other, (sequence_length, ffe)),
                ],
                axis=1,
            )
            gate_pre = dot(h2, gate_w)
            up_pre = dot(h2, up_w)
            grad_hidden = branch_scale * dot_t(cot, down_w)
            sigmoid = jax.nn.sigmoid(gate_pre)
            activated = gate_pre * sigmoid
            hidden = activated * up_pre
            product = hidden * grad_hidden
            dgate_own = jnp.sum(product[:, :ffe], axis=1)
            dgate_other = jnp.sum(product[:, ffe:], axis=1)
            hidden_low = low(weight * hidden)
            weighted = weight * grad_hidden
            grad_gate_pre = low(weighted * up_pre * sigmoid * (1.0 + gate_pre * (1.0 - sigmoid)))
            grad_up_pre = low(weighted * activated)
            mix_row.append(dot(hidden_low, down_w))
            entry_row.append(dot_t(grad_gate_pre, gate_w) + dot_t(grad_up_pre, up_w))
            gate_row.append(
                own_expert[:, None] * dgate_own[None, :]
                + other_expert[:, None] * dgate_other[None, :]
            )
            kept.append((h2, cot, hidden_low, grad_gate_pre, grad_up_pre))
        mix_parts.append(mix_row)
        entry_parts.append(entry_row)
        gate_parts.append(gate_row)

    grad_rows_in = lay.collect(entry_parts, low)
    grad_gates = lay.collect(gate_parts, wide).T
    mixture = lay.collect(mix_parts, low)

    h2_all, cot_all, hidden_all, dgate_all, dup_all = [
        jnp.concatenate(every, axis=0) for every in zip(*kept)
    ]
    expert_sums = []
    for left, right, factor, axis in (
        (h2_all, dgate_all, 1.0, 0),
        (h2_all, dup_all, 1.0, 0),
        (cot_all, hidden_all, branch_scale, 0),
    ):
        both = t_dot(left, right)
        if factor != 1.0:
            both = both * factor
        own = both[:, :ffe] + wide(lay.other_core(low(both[:, ffe:])))
        expert_sums.append(scatter_dp(lay, own, axis))
    grad_gate_out = expert_sums[0][None]
    grad_up_out = expert_sums[1][None]
    grad_down_out = expert_sums[2].T[None]

    result = after_attn + branch_scale * mixture
    grad_result = wide(cotangent)
    grad_logits = gates * (grad_gates - jnp.sum(gates * grad_gates, axis=1, keepdims=True))
    logit_parts = two_parts(grad_logits)
    grad_router = t_dot(normed_two, logit_parts)
    grad_router = grad_router[:, :experts] + grad_router[:, experts:]
    grad_normed_two = grad_rows_in + dot_t(
        logit_parts, jnp.concatenate([router_full, router_full], axis=1)
    )
    grad_gain_two = jnp.sum(grad_normed_two * after_attn * scale_two, axis=0)
    inner_two = grad_normed_two * gain_two
    grad_after = (
        grad_result
        + scale_two * inner_two
        - after_attn * scale_two**3 * jnp.mean(inner_two * after_attn, axis=1, keepdims=True)
    )
    grad_attn_low = low(branch_scale * grad_after)
    grad_out_w = over_dp(lay, attended_low, grad_attn_low)
    attended_gradient = low(back_through(grad_attn_low, out_pieces, q_width)).reshape(
        sequence_length, KEY_VALUE_HEADS, group, HEAD_SIZE
    )
    probs = jnp.exp(masked_scores(query_groups, keys_rot, allowed) - log_total)
    probs_again = low(probs)
    value_gradient = jnp.einsum(
        "hgqk,qhgd->khd", probs_again, attended_gradient, preferred_element_type=jnp.float32
    )
    grad_probs = jnp.einsum(
        "qhgd,khd->hgqk", attended_gradient, value_rows_every, preferred_element_type=jnp.float32
    )
    grad_scores = low(
        probs * (grad_probs - jnp.sum(probs * grad_probs, axis=-1, keepdims=True))
    )
    grad_queries = (
        jnp.einsum(
            "hgqk,khd->qhgd", grad_scores, keys_rot, preferred_element_type=jnp.float32
        ).reshape(sequence_length, QUERY_HEADS, HEAD_SIZE)
        * att_scale
    )
    key_gradient = (
        jnp.einsum("hgqk,qhgd->khd", grad_scores, query_groups, preferred_element_type=jnp.float32)
        * att_scale
    )
    grad_linear = jnp.concatenate(
        [
            low(reverse_rotary(grad_queries, cosine_table, sine_table)).reshape(
                sequence_length, q_width
            ),
            low(reverse_rotary(key_gradient, cosine_table, sine_table)).reshape(
                sequence_length, kv_width
            ),
            low(value_gradient).reshape(sequence_length, kv_width),
        ],
        axis=1,
    )
    grad_qkv_w = over_dp(lay, first_normalized, grad_linear)
    grad_normed_one = back_through(grad_linear, qkv_pieces, width)
    grad_gain_one = jnp.sum(grad_normed_one * tokens_float * scale_one, axis=0)
    inner_one = grad_normed_one * gain_one
    grad_tokens = (
        grad_after
        + scale_one * inner_one
        - tokens_float * scale_one**3 * jnp.mean(inner_one * tokens_float, axis=1, keepdims=True)
    )

    small_grad = jnp.concatenate(
        [grad_router, grad_gain_one[:, None], grad_gain_two[:, None]], axis=1
    )
    small_grad = scatter_dp(lay, small_grad, 0)
    small_grad = jnp.pad(small_grad, ((0, 0), (0, 128 - small_grad.shape[1])))
    first = lax.psum(low(grad_out_w), "expert")
    second = lax.psum(low(jnp.concatenate([grad_qkv_w, small_grad], axis=1)), "expert")
    second = wide(second)
    edge = q_width + 2 * kv_width
    return (
        low(result),
        grad_tokens,
        second[:, :q_width],
        second[:, q_width : q_width + kv_width],
        second[:, q_width + kv_width : edge],
        wide(first),
        second[:, edge : edge + experts],
        second[:, edge + experts],
        second[:, edge + experts + 1],
        grad_gate_out,
        grad_up_out,
        grad_down_out,
    )


def solution(mesh):
    return jax.shard_map(
        body,
        mesh=mesh,
        in_specs=(
            P(("dp", "expert"), None),
            P(("dp", "expert"), None),
            P(("dp", "expert"), None),
            P(("dp", "expert")),
            P("dp", None),
            P("dp", None),
            P("dp", None),
            P("dp", None),
            P("dp", None),
            P("dp"),
            P("dp"),
            P("expert", None, None),
            P("expert", None, None),
            P("expert", None, None),
        ),
        out_specs=(
            P(("dp", "expert"), None),
            P(("dp", "expert"), None),
            P("dp", None),
            P("dp", None),
            P("dp", None),
            P("dp", None),
            P("dp", None),
            P("dp"),
            P("dp"),
            P("expert", "dp", None),
            P("expert", "dp", None),
            P("expert", None, "dp"),
        ),
        check_vma=False,
    )
```

```python
import functools

import jax
import jax.numpy as jnp
from jax import lax
from jax.experimental import pallas as pl
from jax.experimental.pallas import tpu as pltpu
from jax.sharding import PartitionSpec as P

QUERY_HEADS = 24
KEY_VALUE_HEADS = 8
HEAD_SIZE = 64
TOP = 8
RING = 4
LANES = 128
FFE_CHUNKS = 4

eps_norm = 1e-06
att_scale = 0.015625
branch_scale = 0.22
rope_base = 10000.0


def rotation(sequence_length, head_dim):
    half = head_dim // 2
    places = jnp.arange(sequence_length).astype(jnp.float32)[:, None]
    freqs = rope_base ** (-2.0 * jnp.arange(half).astype(jnp.float32) / head_dim)
    angles = places * freqs[None, :]
    return (jnp.cos(angles)[:, None, :], jnp.sin(angles)[:, None, :])


def apply_rotary(values, cosine_table, sine_table):
    half = values.shape[-1] // 2
    first = values[..., :half]
    second = values[..., half:]
    return jnp.concatenate(
        [first * cosine_table - second * sine_table, second * cosine_table + first * sine_table],
        axis=-1,
    )


def reverse_rotary(grads, cosine_table, sine_table):
    half = grads.shape[-1] // 2
    first = grads[..., :half]
    second = grads[..., half:]
    return jnp.concatenate(
        [first * cosine_table + second * sine_table, second * cosine_table - first * sine_table],
        axis=-1,
    )


def masked_scores(query_groups, keys_rot, allowed):
    scores = (
        jnp.einsum("qhgd,khd->hgqk", query_groups, keys_rot, preferred_element_type=jnp.float32)
        * att_scale
    )
    return jnp.where(allowed, scores, -1e30)


def dot(a, b):
    return jnp.dot(a, b, preferred_element_type=jnp.float32)


def dot_t(a, b):
    return lax.dot_general(a, b, (((1,), (1,)), ((), ())), preferred_element_type=jnp.float32)


def t_dot(a, b):
    return lax.dot_general(a, b, (((0,), (0,)), ((), ())), preferred_element_type=jnp.float32)


def low(x):
    return x.astype(jnp.bfloat16)


def wide(x):
    return x.astype(jnp.float32)


def two_parts(x):
    high = low(x)
    return jnp.concatenate([high, low(x - wide(high))], axis=1)


class Layout:
    def __init__(self):
        self.experts = lax.axis_size("expert")
        self.dp = lax.axis_size("dp")
        self.sides = self.experts // (2 * RING)
        self.index = lax.axis_index("expert")
        self.dp_index = lax.axis_index("dp")
        self.core = self.index % 2
        self.side = (self.index // 2) % self.sides
        self.ring = self.index // (2 * self.sides)

    def place(self, ring, side, core):
        return ((ring % RING) * self.sides + side % self.sides) * 2 + core

    def _perm(self, ring, side):
        n = self.experts
        pairs = []
        for i in range(n):
            core, s, r = i % 2, (i // 2) % self.sides, i // (2 * self.sides)
            pairs.append((i, self.place(r + ring, s + side, core)))
        return pairs

    def next_ring(self, x):
        return lax.ppermute(x, "expert", self._perm(1, 0))

    def next_side(self, x):
        return lax.ppermute(x, "expert", self._perm(0, 1))

    def other_core(self, x):
        return lax.ppermute(x, "expert", [(i, i ^ 1) for i in range(self.experts)])

    def next_dp(self, x, step):
        n = self.dp
        return lax.ppermute(x, "dp", [(i, (i + step) % n) for i in range(n)])

    def spread(self, x):
        blocks = []
        for s in range(RING):
            row = [x]
            for _ in range(self.sides - 1):
                row.append(self.next_side(row[-1]))
            blocks.append(row)
            if s < RING - 1:
                x = self.next_ring(x)
        return blocks

    def collect(self, parts):
        total = None
        for s in list(range(1, RING)) + [0]:
            row = parts[s]
            acc = None
            for t in list(range(1, self.sides)) + [0]:
                acc = wide(row[t]) + (0.0 if acc is None else wide(self.next_side(low(acc))))
            total = acc if total is None else wide(self.next_ring(low(total))) + acc
        return total

    def collect_small(self, parts):
        size = parts[0].shape[1] // self.sides
        stacked = jnp.concatenate(parts, axis=0)
        total = stacked[:, :size]
        for t in range(1, self.sides):
            piece = stacked[:, t * size : (t + 1) * size]
            total = total + lax.ppermute(piece, "expert", self._perm(0, -t))
        rows = parts[0].shape[0]
        result = total[:rows]
        for s in range(1, RING):
            piece = total[s * rows : (s + 1) * rows]
            result = result + lax.ppermute(piece, "expert", self._perm(-s, 0))
        return result


def weight_pieces(lay, parts, after):
    rows = parts[0].shape[0]
    half = rows // 2
    start = lay.core * half
    mine = jnp.concatenate(
        [lax.dynamic_slice(w, (start, 0), (half, w.shape[1])) for w in parts], axis=1
    )
    if after is not None:
        mine, _ = lax.optimization_barrier((mine, after))
    own = parts[0] if len(parts) == 1 else jnp.concatenate(parts, axis=1)
    pieces = [(lay.dp_index * rows, own)]
    for step in range(1, lay.dp):
        source = (lay.dp_index - step) % lay.dp
        got = lay.next_dp(mine, step)
        rest = lay.other_core(got)
        pieces.append((source * rows + start, got))
        pieces.append((source * rows + (1 - lay.core) * half, rest))
    return pieces


def through(x, pieces):
    total = None
    for offset, w in pieces:
        part = dot(lax.dynamic_slice(x, (0, offset), (x.shape[0], w.shape[0])), w)
        total = part if total is None else total + part
    return total


def back_through(y, pieces, width):
    out = jnp.zeros((y.shape[0], width), jnp.float32)
    for offset, w in pieces:
        out = lax.dynamic_update_slice(out, dot_t(y, w), (0, offset))
    return out


def features_of(lay, x, step):
    rows = x.shape[1] // lay.dp
    return lax.dynamic_slice(x, (0, ((lay.dp_index + step) % lay.dp) * rows), (x.shape[0], rows))


def over_dp(lay, left, right):
    total = t_dot(features_of(lay, left, 0), right)
    for step in range(1, lay.dp):
        other_left = lay.next_dp(features_of(lay, left, step), step)
        other_right = lay.next_dp(right, step)
        total = total + t_dot(other_left, other_right)
    return total


def scatter_dp(lay, x, axis):
    size = x.shape[axis] // lay.dp

    def part(step):
        start = ((lay.dp_index + step) % lay.dp) * size
        return lax.dynamic_slice_in_dim(x, start, size, axis)

    total = wide(part(0))
    for step in range(1, lay.dp):
        total = total + wide(lay.next_dp(low(part(step)), step))
    return total


def dense_gates(routes, logits):
    experts = logits.shape[1]
    member = jnp.any(
        routes[:, :, None] == jnp.arange(experts, dtype=jnp.int32)[None, None, :], axis=1
    )
    masked = jnp.where(member, logits, -jnp.inf)
    unnormed = jnp.where(member, jnp.exp(logits - jnp.max(masked, axis=1, keepdims=True)), 0.0)
    return unnormed / jnp.sum(unnormed, axis=1, keepdims=True)


def expert_kernel(sides, experts, chunks, aliased, ids, *refs):
    h2_refs, routes_refs = refs[:sides], refs[sides:2*sides]
    refs = refs[2*sides:]
    grad_hidden, router, gate_w, up_w, down_w = refs[:5]
    refs = refs[5 + (4 if aliased else 0):]
    h2_all, hidden_all, dgate_all, dup_all = refs[:4]
    mix_refs, entry_refs = refs[4:4+sides], refs[4+sides:4+2*sides]
    gate_grad = refs[4+2*sides]
    mix_acc, entry_acc, weight_own, weight_other, grad_own, grad_other = refs[5+2*sides:]
    step = pl.program_id(0)
    block = h2_refs[0].shape[0]

    @pl.when(step == 0)
    def _():
        lane = lax.broadcasted_iota(jnp.int32, (block, LANES), 1)
        for t in range(sides):
            rows = slice(t*block, (t+1)*block)
            h2_all[rows, :] = h2_refs[t][...]
            logits = dot(h2_refs[t][...], router[...])
            named = routes_refs[t][...]
            member = named[:, 0:1] == lane
            for k in range(1, named.shape[1]):
                member = member | (named[:, k:k+1] == lane)
            top = jnp.max(jnp.where(member, logits, -1e30), axis=1, keepdims=True)
            unnormed = jnp.where(member, jnp.exp(jnp.minimum(logits - top, 0.0)), 0.0)
            gates = unnormed / jnp.sum(unnormed, axis=1, keepdims=True)
            weight_own[rows, :] = jnp.sum(jnp.where(lane == ids[0], gates, 0.0), axis=1, keepdims=True)
            weight_other[rows, :] = jnp.sum(jnp.where(lane == ids[1], gates, 0.0), axis=1, keepdims=True)
        mix_acc[...] = jnp.zeros_like(mix_acc)
        entry_acc[...] = jnp.zeros_like(entry_acc)
        grad_own[...] = jnp.zeros_like(grad_own)
        grad_other[...] = jnp.zeros_like(grad_other)

    h2 = h2_all[...]
    weight = jnp.where(step < chunks // 2, weight_own[...], weight_other[...])
    gate_pre = dot(h2, gate_w[...])
    up_pre = dot(h2, up_w[...])
    dhid = grad_hidden[...]
    sigmoid = 1.0 / (1.0 + jnp.exp(-gate_pre))
    activated = gate_pre * sigmoid
    hidden = activated * up_pre
    product = hidden * dhid
    partial = product[:, :LANES]
    for k in range(1, product.shape[1] // LANES):
        partial = partial + product[:, k*LANES:(k+1)*LANES]
    weighted = weight * dhid
    hidden_low = low(weight * hidden)
    dgate = low(weighted * up_pre * sigmoid * (1.0 + gate_pre * (1.0 - sigmoid)))
    dup = low(weighted * activated)
    hidden_all[...] = hidden_low
    dgate_all[...] = dgate
    dup_all[...] = dup
    entry_acc[...] += dot_t(dgate, gate_w[...]) + dot_t(dup, up_w[...])
    mix_acc[...] += dot(hidden_low, down_w[...])

    @pl.when(step < chunks // 2)
    def _():
        grad_own[...] += partial
    @pl.when(step >= chunks // 2)
    def _():
        grad_other[...] += partial

    @pl.when(step == chunks - 1)
    def _():
        for t in range(sides):
            rows = slice(t*block, (t+1)*block)
            mix_refs[t][...] = low(mix_acc[rows, :])
            entry_refs[t][...] = low(entry_acc[rows, :])
        lane = lax.broadcasted_iota(jnp.int32, grad_own.shape, 1)
        own = jnp.sum(grad_own[...], axis=1, keepdims=True)
        other = jnp.sum(grad_other[...], axis=1, keepdims=True)
        placed = jnp.where(lane == ids[0], own, 0.0) + jnp.where(lane == ids[1], other, 0.0)
        gate_grad[...] = placed.T[:experts, :]

def expert_stage(s, stages, h2s, routes, grad_hidden, router, weights, ids, experts, bufs):
    sides = len(h2s)
    block, width = h2s[0].shape
    rows = sides*block
    gate_w, up_w, down_w = weights
    both = gate_w.shape[1]
    chunks = FFE_CHUNKS
    size = both // chunks
    whole = lambda shape: pl.BlockSpec(shape, lambda j, ids: (0,)*len(shape))
    in_specs = (
        [whole((block, width))]*sides + [whole(routes[0].shape)]*sides
        + [pl.BlockSpec((rows, size), lambda j, ids: (s, j)),
           whole(router.shape),
           pl.BlockSpec((width, size), lambda j, ids: (0, j)),
           pl.BlockSpec((width, size), lambda j, ids: (0, j)),
           pl.BlockSpec((size, width), lambda j, ids: (j, 0))]
        + ([pl.BlockSpec(memory_space=pl.ANY)]*4 if bufs else []))
    piece = pl.BlockSpec((rows, size), lambda j, ids: (s, j))
    out_specs = ([pl.BlockSpec((rows, width), lambda j, ids: (s, 0)), piece, piece, piece]
        + [whole((block, width))]*(2*sides) + [whole((experts, rows))])
    b16 = jnp.bfloat16
    big = [jax.ShapeDtypeStruct((stages*rows, width), b16)] + [jax.ShapeDtypeStruct((stages*rows, both), b16)]*3
    out_shape = big + [jax.ShapeDtypeStruct((block, width), b16)]*(2*sides) + [jax.ShapeDtypeStruct((experts, rows), jnp.float32)]
    first = 1 + 2*sides + 5
    out = pl.pallas_call(
        functools.partial(expert_kernel, sides, experts, chunks, bool(bufs)),
        out_shape=out_shape,
        grid_spec=pltpu.PrefetchScalarGridSpec(
            num_scalar_prefetch=1, grid=(chunks,), in_specs=in_specs, out_specs=out_specs,
            scratch_shapes=[pltpu.VMEM((rows, width), jnp.float32)]*2
            + [pltpu.VMEM((rows, 1), jnp.float32)]*2 + [pltpu.VMEM((rows, LANES), jnp.float32)]*2),
        input_output_aliases={first+i: i for i in range(4)} if bufs else {},
        name="expert_stage",
        compiler_params=pltpu.CompilerParams(vmem_limit_bytes=56*2**20),
    )(ids, *h2s, *routes, grad_hidden, router, gate_w, up_w, down_w, *(bufs or ()))
    return out[:4], out[4:4+sides], out[4+sides:4+2*sides], out[4+2*sides]

def cot_kernel(sides, aliased, *refs):
    cots = refs[:sides]
    down_w = refs[sides]
    cot_all, grad_hidden = refs[sides+1+(2 if aliased else 0):]
    block = cots[0].shape[0]
    @pl.when(pl.program_id(0) == 0)
    def _():
        for t in range(sides):
            cot_all[t*block:(t+1)*block, :] = cots[t][...]
    grad_hidden[...] = branch_scale * dot_t(cot_all[...], down_w[...])

def cot_stage(s, stages, cots, down_w, bufs):
    sides = len(cots)
    block, width = cots[0].shape
    rows = sides*block
    both = down_w.shape[0]
    size = both // FFE_CHUNKS
    return pl.pallas_call(
        functools.partial(cot_kernel, sides, bool(bufs)),
        out_shape=[jax.ShapeDtypeStruct((stages*rows, width), jnp.bfloat16), jax.ShapeDtypeStruct((stages*rows, both), jnp.float32)],
        grid_spec=pltpu.PrefetchScalarGridSpec(
            num_scalar_prefetch=0, grid=(FFE_CHUNKS,),
            in_specs=[pl.BlockSpec((block, width), lambda j: (0,0))]*sides + [pl.BlockSpec((size, width), lambda j: (j,0))]
            + ([pl.BlockSpec(memory_space=pl.ANY)]*2 if bufs else []),
            out_specs=[pl.BlockSpec((rows, width), lambda j: (s,0)), pl.BlockSpec((rows, size), lambda j: (s,j))]),
        input_output_aliases={sides+1+i: i for i in range(2)} if bufs else {},
        name="cot_stage",
        compiler_params=pltpu.CompilerParams(vmem_limit_bytes=48*2**20),
    )(*cots, down_w, *(bufs or ()))


def body(
    tokens,
    cotangent,
    routes,
    prefix,
    w_query,
    key_projection,
    value_projection,
    w_out,
    w_router,
    norm_attn,
    norm_moe,
    expert_gate,
    expert_up,
    expert_down,
):
    lay = Layout()
    sequence_length, width = tokens.shape
    experts = lay.experts
    group = QUERY_HEADS // KEY_VALUE_HEADS
    rows = w_query.shape[0]

    small = jnp.concatenate([w_router, norm_attn[:, None], norm_moe[:, None]], axis=1)
    small = jnp.pad(small, ((0, 0), (0, LANES - small.shape[1])))
    small_full = jnp.zeros((rows * lay.dp, small.shape[1]), jnp.bfloat16)
    small_full = lax.dynamic_update_slice(small_full, small, (lay.dp_index * rows, 0))
    for step in range(1, lay.dp):
        source = (lay.dp_index - step) % lay.dp
        small_full = lax.dynamic_update_slice(
            small_full, lay.next_dp(small, step), (source * rows, 0)
        )
    router_full = small_full[:, :experts]
    gain_one = wide(small_full[:, experts])[None, :]
    gain_two = wide(small_full[:, experts + 1])[None, :]
    qkv_pieces = weight_pieces(lay, (w_query, key_projection, value_projection), None)
    out_pieces = weight_pieces(lay, (w_out,), qkv_pieces[1][1])

    gate_w = jnp.concatenate([expert_gate[0], lay.other_core(expert_gate[0])], axis=1)
    up_w = jnp.concatenate([expert_up[0], lay.other_core(expert_up[0])], axis=1)
    down_w = jnp.concatenate([expert_down[0], lay.other_core(expert_down[0])], axis=0)

    routes_blocks = lay.spread(routes)
    cot_blocks = lay.spread(cotangent)

    cosine_table, sine_table = rotation(sequence_length, HEAD_SIZE)
    tokens_float = wide(tokens)
    scale_one = lax.rsqrt(jnp.mean(tokens_float * tokens_float, axis=1, keepdims=True) + eps_norm)
    first_normalized = low(tokens_float * scale_one * gain_one)
    linear = through(first_normalized, qkv_pieces)
    q_width = QUERY_HEADS * HEAD_SIZE
    kv_width = KEY_VALUE_HEADS * HEAD_SIZE
    query_linear = linear[:, :q_width].reshape(sequence_length, QUERY_HEADS, HEAD_SIZE)
    key_linear = linear[:, q_width : q_width + kv_width].reshape(
        sequence_length, KEY_VALUE_HEADS, HEAD_SIZE
    )
    value_rows_every = low(linear[:, q_width + kv_width :]).reshape(
        sequence_length, KEY_VALUE_HEADS, HEAD_SIZE
    )
    query_groups = low(apply_rotary(query_linear, cosine_table, sine_table)).reshape(
        sequence_length, KEY_VALUE_HEADS, group, HEAD_SIZE
    )
    keys_rot = low(apply_rotary(key_linear, cosine_table, sine_table))
    query_place = jnp.arange(sequence_length)[:, None]
    key_place = jnp.arange(sequence_length)[None, :]
    allowed = (key_place <= query_place) | (key_place < prefix[0])
    scores = masked_scores(query_groups, keys_rot, allowed)
    highest = jnp.max(scores, axis=-1, keepdims=True)
    unnormed = jnp.exp(scores - highest)
    total = jnp.sum(unnormed, axis=-1, keepdims=True)
    log_total = highest + jnp.log(total)
    probs_low = low(unnormed / total)
    attended = jnp.einsum(
        "hgqk,khd->qhgd", probs_low, value_rows_every, preferred_element_type=jnp.float32
    )
    attended_low = low(attended.reshape(sequence_length, q_width))
    after_attn = tokens_float + branch_scale * through(attended_low, out_pieces)
    scale_two = lax.rsqrt(jnp.mean(after_attn * after_attn, axis=1, keepdims=True) + eps_norm)
    normed_two = low(after_attn * scale_two * gain_two)

    gates = dense_gates(routes, dot(normed_two, router_full))
    h2_blocks = lay.spread(normed_two)
    ids = jnp.stack([lay.index, lay.index + 1 - 2 * lay.core]).astype(jnp.int32)
    ffe = expert_gate.shape[2]

    cot_bufs, bufs = None, None
    for s in range(RING):
        cot_bufs = cot_stage(s, RING, cot_blocks[s], down_w, cot_bufs)
    mix_parts, entry_parts, gate_parts = [], [], []
    for s in range(RING):
        bufs, mix, entry, gate_part = expert_stage(
            s, RING, h2_blocks[s], routes_blocks[s], cot_bufs[1], small_full,
            (gate_w, up_w, down_w), ids, experts, bufs,
        )
        mix_parts.append(mix)
        entry_parts.append(entry)
        gate_parts.append(gate_part)

    grad_rows_in = lay.collect(entry_parts)
    grad_gates = lay.collect_small(gate_parts).T
    mix_parts, grad_rows_in = lax.optimization_barrier((mix_parts, grad_rows_in))
    mixture = lay.collect(mix_parts)

    h2_all, hidden_all, dgate_all, dup_all = bufs
    cot_all = cot_bufs[0]
    expert_sums = []
    for left, right, factor, axis in (
        (h2_all, dgate_all, 1.0, 0),
        (h2_all, dup_all, 1.0, 0),
        (cot_all, hidden_all, branch_scale, 0),
    ):
        both = t_dot(left, right)
        if factor != 1.0:
            both = both * factor
        own = both[:, :ffe] + wide(lay.other_core(low(both[:, ffe:])))
        expert_sums.append(scatter_dp(lay, own, axis))
    grad_gate_out = expert_sums[0][None]
    grad_up_out = expert_sums[1][None]
    grad_down_out = expert_sums[2].T[None]

    result = after_attn + branch_scale * mixture
    grad_result = wide(cotangent)
    grad_logits = gates * (grad_gates - jnp.sum(gates * grad_gates, axis=1, keepdims=True))
    logit_parts = two_parts(grad_logits)
    grad_router = t_dot(normed_two, logit_parts)
    grad_router = grad_router[:, :experts] + grad_router[:, experts:]
    grad_normed_two = grad_rows_in + dot_t(
        logit_parts, jnp.concatenate([router_full, router_full], axis=1)
    )
    grad_gain_two = jnp.sum(grad_normed_two * after_attn * scale_two, axis=0)
    inner_two = grad_normed_two * gain_two
    grad_after = (
        grad_result
        + scale_two * inner_two
        - after_attn * scale_two**3 * jnp.mean(inner_two * after_attn, axis=1, keepdims=True)
    )
    grad_attn_low = low(branch_scale * grad_after)
    grad_out_w = over_dp(lay, attended_low, grad_attn_low)
    attended_gradient = low(back_through(grad_attn_low, out_pieces, q_width)).reshape(
        sequence_length, KEY_VALUE_HEADS, group, HEAD_SIZE
    )
    probs = jnp.exp(masked_scores(query_groups, keys_rot, allowed) - log_total)
    probs_again = low(probs)
    value_gradient = jnp.einsum(
        "hgqk,qhgd->khd", probs_again, attended_gradient, preferred_element_type=jnp.float32
    )
    grad_probs = jnp.einsum(
        "qhgd,khd->hgqk", attended_gradient, value_rows_every, preferred_element_type=jnp.float32
    )
    grad_scores = low(
        probs * (grad_probs - jnp.sum(probs * grad_probs, axis=-1, keepdims=True))
    )
    grad_queries = (
        jnp.einsum(
            "hgqk,khd->qhgd", grad_scores, keys_rot, preferred_element_type=jnp.float32
        ).reshape(sequence_length, QUERY_HEADS, HEAD_SIZE)
        * att_scale
    )
    key_gradient = (
        jnp.einsum("hgqk,qhgd->khd", grad_scores, query_groups, preferred_element_type=jnp.float32)
        * att_scale
    )
    grad_linear = jnp.concatenate(
        [
            low(reverse_rotary(grad_queries, cosine_table, sine_table)).reshape(
                sequence_length, q_width
            ),
            low(reverse_rotary(key_gradient, cosine_table, sine_table)).reshape(
                sequence_length, kv_width
            ),
            low(value_gradient).reshape(sequence_length, kv_width),
        ],
        axis=1,
    )
    grad_qkv_w = over_dp(lay, first_normalized, grad_linear)
    grad_normed_one = back_through(grad_linear, qkv_pieces, width)
    grad_gain_one = jnp.sum(grad_normed_one * tokens_float * scale_one, axis=0)
    inner_one = grad_normed_one * gain_one
    grad_tokens = (
        grad_after
        + scale_one * inner_one
        - tokens_float * scale_one**3 * jnp.mean(inner_one * tokens_float, axis=1, keepdims=True)
    )

    small_grad = jnp.concatenate(
        [grad_router, grad_gain_one[:, None], grad_gain_two[:, None]], axis=1
    )
    small_grad = scatter_dp(lay, small_grad, 0)
    small_grad = jnp.pad(small_grad, ((0, 0), (0, 128 - small_grad.shape[1])))
    first = lax.psum(low(grad_out_w), "expert")
    second = low(jnp.concatenate([grad_qkv_w, small_grad], axis=1))
    second, first = lax.optimization_barrier((second, first))
    second = wide(lax.psum(second, "expert"))
    edge = q_width + 2 * kv_width
    return (
        low(result),
        grad_tokens,
        second[:, :q_width],
        second[:, q_width : q_width + kv_width],
        second[:, q_width + kv_width : edge],
        wide(first),
        second[:, edge : edge + experts],
        second[:, edge + experts],
        second[:, edge + experts + 1],
        grad_gate_out,
        grad_up_out,
        grad_down_out,
    )


def solution(mesh):
    return jax.shard_map(
        body,
        mesh=mesh,
        in_specs=(
            P(("dp", "expert"), None),
            P(("dp", "expert"), None),
            P(("dp", "expert"), None),
            P(("dp", "expert")),
            P("dp", None),
            P("dp", None),
            P("dp", None),
            P("dp", None),
            P("dp", None),
            P("dp"),
            P("dp"),
            P("expert", None, None),
            P("expert", None, None),
            P("expert", None, None),
        ),
        out_specs=(
            P(("dp", "expert"), None),
            P(("dp", "expert"), None),
            P("dp", None),
            P("dp", None),
            P("dp", None),
            P("dp", None),
            P("dp", None),
            P("dp"),
            P("dp"),
            P("expert", "dp", None),
            P("expert", "dp", None),
            P("expert", None, "dp"),
        ),
        check_vma=False,
    )
```
